32 devices in a mesh: depth: 4 (over y, x), tile: 8 (over z, core).
Axes of the slice: x: 2, y: 2, z: 4, core: 2. Of those that a mesh axis runs over, the one named last changes fastest.
Arguments:
- volume: float32 [32, 64, 256], P('depth', 'tile'), may hold values from 0.01 to 4
- measured: float32 [128, 64, 256], P('depth', 'tile'), may hold values from 0.3 to 3
- point_spread: bfloat16 [11, 11, 32, 128], replicated, may hold values from 6.25e-05 to 1.125
Outputs:
- updated: float32 [32, 64, 256], P('depth', 'tile')
The draws below stay inside these ranges and needn't reach their ends.
All inputs are finite; a program needn't handle non-finite values.
Results may differ from the reference program's by a relative error of at most 0.0008.
Values may be sent and summed in bfloat16 or wider, within the bound.
A program may use at most 64 MiB of HBM per device.

```python
import math
import jax
import jax.numpy as jnp
from jax import lax

VIEWS = 128
PSF_RADIUS = 5
NX = 256
PLANES = 32
NY = 64


def log_spread(key, full_shape, lowest, highest):
    return jnp.exp(jax.random.uniform(key, full_shape, jnp.float32, math.log(lowest), math.log(highest)))


def draw_volume(key, part):
    key_list = jax.random.split(jax.random.fold_in(key, 7), 3)
    full_shape = (PLANES, NY, NX)
    bead_picks = jax.random.randint(key_list[0], full_shape, 0, 50)
    background = log_spread(key_list[1], full_shape, 0.02, 0.08)
    bright = log_spread(key_list[2], full_shape, 1.0, 3.0)
    return jnp.where(bead_picks == 0, bright, background).astype(jnp.float32)


def draw_point_spread(key, part):
    extent = 2 * PSF_RADIUS + 1
    key_list = jax.random.split(jax.random.fold_in(key, 13), 4)
    view_tilt = jax.random.uniform(key_list[0], (2, 1, VIEWS), jnp.float32, -1.0, 1.0)
    jitter = jax.random.uniform(key_list[1], (PLANES,), jnp.float32, -0.5, 0.5)
    levels = ((jnp.arange(PLANES, dtype=jnp.float32) + 0.5 + jitter) * 2.0 / PLANES - 1.0)[:, None]
    centers = (PSF_RADIUS - 0.5) * levels[None] * view_tilt
    blob_width = 0.35 + 0.45 * jnp.abs(levels)
    offsets = (jnp.arange(extent, dtype=jnp.float32) - PSF_RADIUS)[:, None, None]
    row_part = jnp.exp(-0.5 * ((offsets - centers[0][None]) / blob_width[None]) ** 2)
    col_part = jnp.exp(-0.5 * ((offsets - centers[1][None]) / blob_width[None]) ** 2)
    blob_shape = row_part[:, None] * col_part[None, :]
    blob_shape = blob_shape / jnp.sum(blob_shape, axis=(0, 1), keepdims=True)
    amplitude = log_spread(key_list[2], (PLANES, VIEWS), 0.5, 2.0)
    texture = log_spread(key_list[3], (extent, extent, PLANES, VIEWS), 0.7, 1.4)
    spread_kernel = 12.5 / PLANES * amplitude[None, None] * texture * (blob_shape + 0.0005)
    return spread_kernel.astype(jnp.bfloat16)


def block_scale(rng, shape, pieces, least, high):
    def one(position, shards_of):
        draws = jax.random.uniform(jax.random.fold_in(jax.random.fold_in(rng, 6), position), (shards_of,), jnp.float32, least / len(pieces), high / len(pieces))
        return jnp.repeat(jnp.exp(draws), shape[position] // shards_of).reshape((-1,) + (1,) * (len(shape) - position - 1))

    level = one(*pieces[0])
    for cut in pieces[1:]:
        level = level * one(*cut)
    return level


def setup_inputs(seed: int = 0) -> dict:
    keys = jax.random.split(jax.random.key(seed), 4)
    return {
        "volume": draw_volume(jax.random.fold_in(keys[3], 71), 0),
        "measured": jnp.clip(jnp.exp(math.log(3.0) - 2.3025851 * jax.random.uniform(keys[1], (VIEWS, NY, NX), jnp.float32) ** block_scale(keys[1], (VIEWS, NY, NX), ((0, 4), (1, 8)), -0.2, 0.2)), 0.3, 3.0),
        "point_spread": draw_point_spread(jax.random.fold_in(keys[3], 71), 0),
    }


def reference(volume, measured, point_spread):
    extent = 2 * PSF_RADIUS + 1
    height = volume.shape[1]
    breadth = volume.shape[2]
    kernel = point_spread.astype(jnp.float32)
    volume_low = volume.astype(jnp.bfloat16)
    volume_low = lax.optimization_barrier(volume_low).astype(jnp.float32)
    padded = jnp.pad(volume_low, ((0, 0), (PSF_RADIUS, PSF_RADIUS), (PSF_RADIUS, PSF_RADIUS)))
    projection = jnp.zeros(measured.shape, jnp.float32)
    for row_shift in range(extent):
        for col_shift in range(extent):
            window = padded[:, row_shift:row_shift + height, col_shift:col_shift + breadth]
            projection = projection + jnp.einsum("zyx,zv->vyx", window, kernel[row_shift, col_shift], precision=lax.Precision.HIGHEST)
    ratio = (measured / projection).astype(jnp.bfloat16)
    ratio = lax.optimization_barrier(ratio).astype(jnp.float32)
    padded_ratio = jnp.pad(ratio, ((0, 0), (PSF_RADIUS, PSF_RADIUS), (PSF_RADIUS, PSF_RADIUS)))
    back_sum = jnp.zeros(volume.shape, jnp.float32)
    for row_shift in range(extent):
        for col_shift in range(extent):
            window = padded_ratio[:, row_shift:row_shift + height, col_shift:col_shift + breadth]
            tap_weights = kernel[extent - 1 - row_shift, extent - 1 - col_shift]
            back_sum = back_sum + jnp.einsum("vyx,zv->zyx", window, tap_weights, precision=lax.Precision.HIGHEST)
    weight = jnp.sum(kernel, axis=(0, 1, 3))
    return volume * back_sum / weight[:, None, None]
```

```python
import functools

import jax
import jax.numpy as jnp
from jax import lax
from jax.experimental import pallas as pl
from jax.experimental.pallas import tpu as pltpu
from jax.sharding import PartitionSpec as P

MESH = pl.DeviceIdType.MESH
F32 = jnp.float32
BF16 = jnp.bfloat16


def shifted_sum(products, taps, stride, used, sign):
    radius = taps // 2
    width = products.shape[1]
    lanes = lax.broadcasted_iota(jnp.int32, (used, width), 1)
    total = products[radius * stride : radius * stride + used]
    for b in range(taps):
        if b == radius:
            continue
        move = sign * (b - radius)
        piece = pltpu.roll(products[b * stride : b * stride + used], move % width, 1)
        keep = lanes >= move if move > 0 else lanes < width + move
        total = total + jnp.where(keep, piece, 0.0)
    return total


def kernel(
    count_d, count_t, views,
    vol_hbm, meas_hbm, ps_hbm, out_ref,
    vol_v, meas_v, ps_v, gathered, slab_v, w_fwd, w_back, ratio_v, part_v, part_in, weight_v,
    load_sem, gather_send, gather_recv, halo_send, halo_recv, sum_send, sum_recv,
):
    taps = ps_hbm.shape[0]
    radius = taps // 2
    planes_all, views_all = ps_hbm.shape[2:]
    planes, rows, width = vol_hbm.shape
    vpad = ratio_v.shape[1]
    my_d = lax.axis_index("depth")
    my_t = lax.axis_index("tile")
    has_prev = my_t > 0
    has_next = my_t < count_t - 1

    load_vol = pltpu.make_async_copy(vol_hbm, vol_v, load_sem.at[0])
    load_ps = pltpu.make_async_copy(ps_hbm, ps_v, load_sem.at[1])
    load_meas = pltpu.make_async_copy(meas_hbm, meas_v, load_sem.at[2])
    load_vol.start()
    load_ps.start()
    load_meas.start()

    def peer(k):
        return lax.rem(my_d + k, count_d)

    barrier = pltpu.get_barrier_semaphore()

    def greet(k, move):
        pl.semaphore_signal(
            barrier, inc=1, device_id={"depth": peer(k), "tile": my_t + move}, device_id_type=MESH
        )

    for k in range(1, count_d):
        greet(k, 0)

    @pl.when(has_prev)
    def _():
        for k in range(count_d):
            greet(k, -1)

    @pl.when(has_next)
    def _():
        for k in range(count_d):
            greet(k, 1)

    @pl.when(jnp.logical_not(has_prev))
    def _():
        gathered[:, :radius] = jnp.zeros((count_d, radius, planes, width), BF16)
        ratio_v[:radius] = jnp.zeros((radius, vpad, width), BF16)

    @pl.when(jnp.logical_not(has_next))
    def _():
        gathered[:, radius + rows :] = jnp.zeros((count_d, radius, planes, width), BF16)
        ratio_v[radius + rows :] = jnp.zeros((radius, vpad, width), BF16)

    load_vol.wait()
    for y in range(rows):
        gathered[my_d, radius + y] = vol_v[:, y, :].astype(BF16)

    takes = (pl.ds(radius, rows), pl.ds(rows, radius), pl.ds(radius, radius))
    puts = (pl.ds(radius, rows), pl.ds(0, radius), pl.ds(radius + rows, radius))
    moves = (0, 1, -1)

    def gather_out(kind, k):
        return pltpu.make_async_remote_copy(
            src_ref=gathered.at[my_d, takes[kind]],
            dst_ref=gathered.at[my_d, puts[kind]],
            send_sem=gather_send.at[kind, k],
            recv_sem=gather_recv.at[kind, k],
            device_id={"depth": peer(k), "tile": my_t + moves[kind]},
            device_id_type=MESH,
        )

    def gather_in(kind, k):
        source = lax.rem(my_d + count_d - k, count_d)
        return pltpu.make_async_remote_copy(
            src_ref=gathered.at[source, puts[kind]],
            dst_ref=gathered.at[source, puts[kind]],
            send_sem=gather_send.at[kind, k],
            recv_sem=gather_recv.at[kind, k],
            device_id={"depth": peer(k), "tile": my_t + moves[kind]},
            device_id_type=MESH,
        )

    pl.semaphore_wait(
        barrier,
        count_d * (1 + has_prev.astype(jnp.int32) + has_next.astype(jnp.int32)) - 1,
    )
    for k in range(1, count_d):
        gather_out(0, k).start()

    @pl.when(has_next)
    def _():
        for k in range(count_d):
            gather_out(1, k).start()

    @pl.when(has_prev)
    def _():
        for k in range(count_d):
            gather_out(2, k).start()

    load_ps.wait()
    row_id = lax.broadcasted_iota(jnp.int32, (vpad, views_all), 0)
    col_id = lax.broadcasted_iota(jnp.int32, (vpad, views_all), 1)
    pick = jnp.where((col_id == my_d * views + row_id) & (row_id < views), 1.0, 0.0).astype(BF16)
    for b in range(taps):
        table = ps_v[:, b].reshape(taps * planes_all, views_all)
        w_fwd[b * vpad : (b + 1) * vpad, :] = lax.dot_general(
            pick, table, (((1,), (1,)), ((), ())), preferred_element_type=F32
        ).astype(BF16)
    lanes = 128
    group = lanes // vpad
    from_id = lax.broadcasted_iota(jnp.int32, (views_all, lanes), 0)
    to_id = lax.broadcasted_iota(jnp.int32, (views_all, lanes), 1)
    for first in range(0, taps, group):
        placed = None
        for slot in range(min(group, taps - first)):
            offset = to_id - slot * vpad
            place = jnp.where(
                (from_id == my_d * views + offset) & (offset >= 0) & (offset < views), 1.0, 0.0
            ).astype(BF16)
            table = ps_v[taps - 1 - first - slot].reshape(taps * planes_all, views_all)
            term = jnp.dot(table, place, preferred_element_type=F32)
            placed = term if placed is None else placed + term
        w_back[:, first * vpad : first * vpad + lanes] = placed.astype(BF16)
    spread = jnp.zeros((planes_all, views_all), F32)
    for a in range(taps):
        for b in range(taps):
            spread = spread + ps_v[a, b].astype(F32)
    weight_v[...] = jnp.broadcast_to(
        jnp.sum(spread, axis=1, keepdims=True), (planes_all, width)
    )
    load_meas.wait()

    for k in range(1, count_d):
        gather_in(0, k).wait_recv()

    @pl.when(has_prev)
    def _():
        for k in range(count_d):
            gather_in(1, k).wait_recv()

    @pl.when(has_next)
    def _():
        for k in range(count_d):
            gather_in(2, k).wait_recv()

    for r in range(rows + 2 * radius):
        slab_v[r] = jnp.concatenate(
            [gathered[d, r].astype(F32) for d in range(count_d)], axis=0
        ).astype(BF16)

    def halo(up):
        take, put = (pl.ds(radius, radius), pl.ds(radius + rows, radius)) if up else (
            pl.ds(rows, radius), pl.ds(0, radius)
        )
        return pltpu.make_async_remote_copy(
            src_ref=ratio_v.at[take],
            dst_ref=ratio_v.at[put],
            send_sem=halo_send.at[int(up)],
            recv_sem=halo_recv.at[int(up)],
            device_id={"depth": my_d, "tile": my_t - 1 if up else my_t + 1},
            device_id_type=MESH,
        )

    for y in range(rows):
        products = jnp.dot(
            w_fwd[...],
            slab_v[y : y + taps].reshape(taps * planes_all, width),
            preferred_element_type=F32,
        )
        projection = shifted_sum(products, taps, vpad, views, -1)
        ratio = meas_v[:, y, :] / projection
        if vpad > views:
            ratio = jnp.concatenate([ratio, jnp.zeros((vpad - views, width), F32)], axis=0)
        ratio_v[radius + y] = ratio.astype(BF16)
        if y == radius - 1:
            @pl.when(has_prev)
            def _():
                halo(True).start()

    @pl.when(has_next)
    def _():
        halo(False).start()
        halo(True).wait_recv()

    @pl.when(has_prev)
    def _():
        halo(False).wait_recv()

    half = rows // 2

    def part_out(piece, k):
        return pltpu.make_async_remote_copy(
            src_ref=part_v.at[peer(k), pl.ds(piece * half, half)],
            dst_ref=part_in.at[k, pl.ds(piece * half, half)],
            send_sem=sum_send.at[piece, k],
            recv_sem=sum_recv.at[piece, k],
            device_id={"depth": peer(k), "tile": my_t},
            device_id_type=MESH,
        )

    for y in range(rows):
        products = jnp.dot(
            w_back[:, : taps * vpad],
            ratio_v[y : y + taps].reshape(taps * vpad, width),
            preferred_element_type=F32,
        )
        back = shifted_sum(products, taps, planes_all, planes_all, 1)
        for d in range(count_d):
            part_v[d, y] = back[d * planes : (d + 1) * planes]
        if (y + 1) % half == 0:
            for k in range(1, count_d):
                part_out(y // half, k).start()

    weight = weight_v[pl.ds(pl.multiple_of(my_d * planes, planes), planes), :]
    for piece in range(2):
        for k in range(1, count_d):
            part_out(piece, k).wait_recv()
        for y in range(piece * half, (piece + 1) * half):
            total = part_v[my_d, y]
            for k in range(1, count_d):
                total = total + part_in[k, y]
            out_ref[:, y, :] = total / weight

    for k in range(1, count_d):
        gather_out(0, k).wait_send()
        part_out(0, k).wait_send()
        part_out(1, k).wait_send()

    @pl.when(has_next)
    def _():
        for k in range(count_d):
            gather_out(1, k).wait_send()
        halo(False).wait_send()

    @pl.when(has_prev)
    def _():
        for k in range(count_d):
            gather_out(2, k).wait_send()
        halo(True).wait_send()


def body(count_d, count_t, volume, measured, point_spread):
    planes, rows, width = volume.shape
    views = measured.shape[0]
    taps = point_spread.shape[0]
    radius = taps // 2
    planes_all = point_spread.shape[2]
    vpad = -(-views // 16) * 16
    group = 128 // vpad
    tall = rows + 2 * radius
    anywhere = pl.BlockSpec(memory_space=pl.ANY)
    scaled = pl.pallas_call(
        functools.partial(kernel, count_d, count_t, views),
        out_shape=jax.ShapeDtypeStruct(volume.shape, F32),
        in_specs=[anywhere] * 3,
        out_specs=pl.BlockSpec(memory_space=pltpu.VMEM),
        scratch_shapes=[
            pltpu.VMEM(volume.shape, F32),
            pltpu.VMEM(measured.shape, F32),
            pltpu.VMEM(point_spread.shape, BF16),
            pltpu.VMEM((count_d, tall, planes, width), BF16),
            pltpu.VMEM((tall, planes_all, width), BF16),
            pltpu.VMEM((taps * vpad, taps * planes_all), BF16),
            pltpu.VMEM((taps * planes_all, -(-taps // group) * 128), BF16),
            pltpu.VMEM((tall, vpad, width), BF16),
            pltpu.VMEM((count_d, rows, planes, width), F32),
            pltpu.VMEM((count_d, rows, planes, width), F32),
            pltpu.VMEM((planes_all, width), F32),
            pltpu.SemaphoreType.DMA((3,)),
            pltpu.SemaphoreType.DMA((3, count_d)),
            pltpu.SemaphoreType.DMA((3, count_d)),
            pltpu.SemaphoreType.DMA((2,)),
            pltpu.SemaphoreType.DMA((2,)),
            pltpu.SemaphoreType.DMA((2, count_d)),
            pltpu.SemaphoreType.DMA((2, count_d)),
        ],
        compiler_params=pltpu.CompilerParams(collective_id=0, has_side_effects=True),
    )(volume, measured, point_spread)
    return volume * scaled


def solution(mesh):
    in_specs = (P("depth", "tile", None), P("depth", "tile", None), P())
    out_specs = P("depth", "tile", None)
    run = functools.partial(body, mesh.shape["depth"], mesh.shape["tile"])
    return jax.shard_map(run, mesh=mesh, in_specs=in_specs, out_specs=out_specs, check_vma=False)
```

```python
import functools

import jax
import jax.numpy as jnp
from jax import lax
from jax.experimental import pallas as pl
from jax.experimental.pallas import tpu as pltpu
from jax.sharding import PartitionSpec as P

MESH = pl.DeviceIdType.MESH
F32 = jnp.float32
BF16 = jnp.bfloat16
PIECES = 4


def shifted_sum(products, taps, stride, used, sign):
    radius = taps // 2
    width = products.shape[1]
    lanes = lax.broadcasted_iota(jnp.int32, (used, width), 1)
    total = products[radius * stride : radius * stride + used]
    for b in range(taps):
        if b == radius:
            continue
        move = sign * (b - radius)
        piece = pltpu.roll(products[b * stride : b * stride + used], move % width, 1)
        keep = lanes >= move if move > 0 else lanes < width + move
        total = total + jnp.where(keep, piece, 0.0)
    return total


def kernel(
    count_d, count_t, views,
    vol_hbm, meas_hbm, ps_hbm, out_ref,
    vol_v, meas_v, ps_v, gathered, slab_v, w_fwd, w_back, ratio_v, part_v, part_in, back_v,
    scaled_v, load_sem, gather_send, gather_recv, halo_send, halo_recv, sum_send, sum_recv,
):
    taps = ps_hbm.shape[0]
    radius = taps // 2
    planes_all, views_all = ps_hbm.shape[2:]
    planes, rows, width = vol_hbm.shape
    vpad = ratio_v.shape[1]
    my_d = lax.axis_index("depth")
    my_t = lax.axis_index("tile")
    has_prev = my_t > 0
    has_next = my_t < count_t - 1

    load_vol = pltpu.make_async_copy(vol_hbm, vol_v, load_sem.at[0])
    load_ps = pltpu.make_async_copy(ps_hbm, ps_v, load_sem.at[1])
    load_meas = pltpu.make_async_copy(meas_hbm, meas_v, load_sem.at[2])
    load_vol.start()
    load_ps.start()
    load_meas.start()

    def peer(k):
        return lax.rem(my_d + k, count_d)

    barrier = pltpu.get_barrier_semaphore()

    def greet(k, move):
        pl.semaphore_signal(
            barrier, inc=1, device_id={"depth": peer(k), "tile": my_t + move}, device_id_type=MESH
        )

    for k in range(1, count_d):
        greet(k, 0)

    @pl.when(has_prev)
    def _():
        for k in range(count_d):
            greet(k, -1)

    @pl.when(has_next)
    def _():
        for k in range(count_d):
            greet(k, 1)

    @pl.when(jnp.logical_not(has_prev))
    def _():
        gathered[:, :radius] = jnp.zeros((count_d, radius, planes, width), BF16)
        ratio_v[:radius] = jnp.zeros((radius, vpad, width), BF16)

    @pl.when(jnp.logical_not(has_next))
    def _():
        gathered[:, radius + rows :] = jnp.zeros((count_d, radius, planes, width), BF16)
        ratio_v[radius + rows :] = jnp.zeros((radius, vpad, width), BF16)

    load_vol.wait()
    for y in range(rows):
        gathered[my_d, radius + y] = vol_v[:, y, :].astype(BF16)

    takes = (pl.ds(radius, rows), pl.ds(rows, radius), pl.ds(radius, radius))
    puts = (pl.ds(radius, rows), pl.ds(0, radius), pl.ds(radius + rows, radius))
    moves = (0, 1, -1)

    def gather_out(kind, k):
        return pltpu.make_async_remote_copy(
            src_ref=gathered.at[my_d, takes[kind]],
            dst_ref=gathered.at[my_d, puts[kind]],
            send_sem=gather_send.at[kind, k],
            recv_sem=gather_recv.at[kind, k],
            device_id={"depth": peer(k), "tile": my_t + moves[kind]},
            device_id_type=MESH,
        )

    def gather_in(kind, k):
        source = lax.rem(my_d + count_d - k, count_d)
        return pltpu.make_async_remote_copy(
            src_ref=gathered.at[source, puts[kind]],
            dst_ref=gathered.at[source, puts[kind]],
            send_sem=gather_send.at[kind, k],
            recv_sem=gather_recv.at[kind, k],
            device_id={"depth": peer(k), "tile": my_t + moves[kind]},
            device_id_type=MESH,
        )

    pl.semaphore_wait(
        barrier,
        count_d * (1 + has_prev.astype(jnp.int32) + has_next.astype(jnp.int32)) - 1,
    )
    for k in range(1, count_d):
        gather_out(0, k).start()

    @pl.when(has_next)
    def _():
        for k in range(count_d):
            gather_out(1, k).start()

    @pl.when(has_prev)
    def _():
        for k in range(count_d):
            gather_out(2, k).start()

    load_ps.wait()
    row_id = lax.broadcasted_iota(jnp.int32, (vpad, views_all), 0)
    col_id = lax.broadcasted_iota(jnp.int32, (vpad, views_all), 1)
    pick = jnp.where((col_id == my_d * views + row_id) & (row_id < views), 1.0, 0.0).astype(BF16)
    for b in range(taps):
        table = ps_v[:, b].reshape(taps * planes_all, views_all)
        w_fwd[b * vpad : (b + 1) * vpad, :] = lax.dot_general(
            pick, table, (((1,), (1,)), ((), ())), preferred_element_type=F32
        ).astype(BF16)
    lanes = 128
    group = lanes // vpad
    from_id = lax.broadcasted_iota(jnp.int32, (views_all, lanes), 0)
    to_id = lax.broadcasted_iota(jnp.int32, (views_all, lanes), 1)
    for first in range(0, taps, group):
        placed = None
        for slot in range(min(group, taps - first)):
            offset = to_id - slot * vpad
            place = jnp.where(
                (from_id == my_d * views + offset) & (offset >= 0) & (offset < views), 1.0, 0.0
            ).astype(BF16)
            table = ps_v[taps - 1 - first - slot].reshape(taps * planes_all, views_all)
            term = jnp.dot(table, place, preferred_element_type=F32)
            placed = term if placed is None else placed + term
        w_back[:, first * vpad : first * vpad + lanes] = placed.astype(BF16)
    spread = jnp.zeros((planes_all, views_all), F32)
    for a in range(taps):
        for b in range(taps):
            spread = spread + ps_v[a, b].astype(F32)
    scale = 1.0 / jnp.sum(spread, axis=1, keepdims=True)
    load_meas.wait()

    for k in range(1, count_d):
        gather_in(0, k).wait_recv()

    @pl.when(has_prev)
    def _():
        for k in range(count_d):
            gather_in(1, k).wait_recv()

    @pl.when(has_next)
    def _():
        for k in range(count_d):
            gather_in(2, k).wait_recv()

    for r in range(rows + 2 * radius):
        slab_v[r] = jnp.concatenate(
            [gathered[d, r].astype(F32) for d in range(count_d)], axis=0
        ).astype(BF16)

    def halo(up, piece):
        first, size = up_pieces[piece] if up else down_pieces[piece]
        take = pl.ds(radius + first, size)
        put = pl.ds(radius + first + (rows if up else -rows), size)
        return pltpu.make_async_remote_copy(
            src_ref=ratio_v.at[take],
            dst_ref=ratio_v.at[put],
            send_sem=halo_send.at[int(up), piece],
            recv_sem=halo_recv.at[int(up), piece],
            device_id={"depth": my_d, "tile": my_t - 1 if up else my_t + 1},
            device_id_type=MESH,
        )

    cut = (radius + 1) // 2
    up_pieces = ((0, cut), (cut, radius - cut))
    down_pieces = ((rows - radius, radius - cut), (rows - cut, cut))

    for y in range(rows):
        products = jnp.dot(
            w_fwd[...],
            slab_v[y : y + taps].reshape(taps * planes_all, width),
            preferred_element_type=F32,
        )
        projection = shifted_sum(products, taps, vpad, views, -1)
        ratio = meas_v[:, y, :] / projection
        if vpad > views:
            ratio = jnp.concatenate([ratio, jnp.zeros((vpad - views, width), F32)], axis=0)
        ratio_v[radius + y] = ratio.astype(BF16)
        ends_up = [i for i in range(2) if y + 1 == sum(up_pieces[i])]
        ends_down = [i for i in range(2) if y + 1 == sum(down_pieces[i])]
        if ends_up:
            @pl.when(has_prev)
            def _():
                halo(True, ends_up[0]).start()
        if ends_down:
            @pl.when(has_next)
            def _():
                halo(False, ends_down[0]).start()

    @pl.when(has_next)
    def _():
        halo(True, 0).wait_recv()
        halo(True, 1).wait_recv()

    @pl.when(has_prev)
    def _():
        halo(False, 0).wait_recv()
        halo(False, 1).wait_recv()

    half = rows // PIECES

    def part_out(piece, k):
        return pltpu.make_async_remote_copy(
            src_ref=part_v.at[peer(k), pl.ds(piece * half, half)],
            dst_ref=part_in.at[k, pl.ds(piece * half, half)],
            send_sem=sum_send.at[piece, k],
            recv_sem=sum_recv.at[piece, k],
            device_id={"depth": peer(k), "tile": my_t},
            device_id_type=MESH,
        )

    for y in range(rows):
        products = jnp.dot(
            w_back[:, : taps * vpad],
            ratio_v[y : y + taps].reshape(taps * vpad, width),
            preferred_element_type=F32,
        )
        back = shifted_sum(products, taps, planes_all, planes_all, 1) * scale
        back_v[y] = back
        for d in range(count_d):
            part_v[d, y] = back[d * planes : (d + 1) * planes]
        if (y + 1) % half == 0:
            for k in range(1, count_d):
                part_out(y // half, k).start()

    own = pl.ds(pl.multiple_of(my_d * planes, planes), planes)
    for piece in range(PIECES):
        for k in range(1, count_d):
            part_out(piece, k).wait_recv()
        for y in range(piece * half, (piece + 1) * half):
            total = back_v[y, own]
            for k in range(1, count_d):
                total = total + part_in[k, y]
            scaled_v[:, y, :] = total
    store = pltpu.make_async_copy(scaled_v, out_ref, load_sem.at[3])
    store.start()

    for k in range(1, count_d):
        gather_out(0, k).wait_send()
        for piece in range(PIECES):
            part_out(piece, k).wait_send()

    @pl.when(has_next)
    def _():
        for k in range(count_d):
            gather_out(1, k).wait_send()
        halo(False, 0).wait_send()
        halo(False, 1).wait_send()

    @pl.when(has_prev)
    def _():
        for k in range(count_d):
            gather_out(2, k).wait_send()
        halo(True, 0).wait_send()
        halo(True, 1).wait_send()

    store.wait()


def body(count_d, count_t, volume, measured, point_spread):
    planes, rows, width = volume.shape
    views = measured.shape[0]
    taps = point_spread.shape[0]
    radius = taps // 2
    planes_all = point_spread.shape[2]
    vpad = -(-views // 16) * 16
    group = 128 // vpad
    tall = rows + 2 * radius
    anywhere = pl.BlockSpec(memory_space=pl.ANY)
    scaled = pl.pallas_call(
        functools.partial(kernel, count_d, count_t, views),
        out_shape=jax.ShapeDtypeStruct(volume.shape, F32),
        in_specs=[pl.BlockSpec(memory_space=pltpu.HBM)] * 3,
        out_specs=anywhere,
        scratch_shapes=[
            pltpu.VMEM(volume.shape, F32),
            pltpu.VMEM(measured.shape, F32),
            pltpu.VMEM(point_spread.shape, BF16),
            pltpu.VMEM((count_d, tall, planes, width), BF16),
            pltpu.VMEM((tall, planes_all, width), BF16),
            pltpu.VMEM((taps * vpad, taps * planes_all), BF16),
            pltpu.VMEM((taps * planes_all, -(-taps // group) * 128), BF16),
            pltpu.VMEM((tall, vpad, width), BF16),
            pltpu.VMEM((count_d, rows, planes, width), F32),
            pltpu.VMEM((count_d, rows, planes, width), F32),
            pltpu.VMEM((rows, planes_all, width), F32),
            pltpu.VMEM(volume.shape, F32),
            pltpu.SemaphoreType.DMA((4,)),
            pltpu.SemaphoreType.DMA((3, count_d)),
            pltpu.SemaphoreType.DMA((3, count_d)),
            pltpu.SemaphoreType.DMA((2, 2)),
            pltpu.SemaphoreType.DMA((2, 2)),
            pltpu.SemaphoreType.DMA((PIECES, count_d)),
            pltpu.SemaphoreType.DMA((PIECES, count_d)),
        ],
        compiler_params=pltpu.CompilerParams(
            collective_id=0, has_side_effects=True, vmem_limit_bytes=32 * 2**20
        ),
    )(volume, measured, point_spread)
    return volume * scaled


def solution(mesh):
    in_specs = (P("depth", "tile", None), P("depth", "tile", None), P())
    out_specs = P("depth", "tile", None)
    run = functools.partial(body, mesh.shape["depth"], mesh.shape["tile"])
    return jax.shard_map(run, mesh=mesh, in_specs=in_specs, out_specs=out_specs, check_vma=False)
```

```python
import functools

import jax
import jax.numpy as jnp
from jax import lax
from jax.experimental import pallas as pl
from jax.experimental.pallas import tpu as pltpu
from jax.sharding import PartitionSpec as P

MESH = pl.DeviceIdType.MESH
F32 = jnp.float32
BF16 = jnp.bfloat16
PIECES = 4


def shifted_sum(products, taps, stride, used, sign):
    radius = taps // 2
    width = products.shape[1]
    lanes = lax.broadcasted_iota(jnp.int32, (used, width), 1)
    total = products[radius * stride : radius * stride + used]
    for b in range(taps):
        if b == radius:
            continue
        move = sign * (b - radius)
        piece = pltpu.roll(products[b * stride : b * stride + used], move % width, 1)
        keep = lanes >= move if move > 0 else lanes < width + move
        total = total + jnp.where(keep, piece, 0.0)
    return total


def kernel(
    count_d, count_t, views,
    vol_hbm, meas_hbm, ps_hbm, out_ref,
    vol_v, meas_v, ps_v, gathered, slab_v, w_fwd, w_back, ratio_v, part_v, part_in, back_v,
    scaled_v, load_sem, gather_send, gather_recv, halo_send, halo_recv, sum_send, sum_recv,
):
    taps = ps_hbm.shape[0]
    radius = taps // 2
    planes_all, views_all = ps_hbm.shape[2:]
    planes, rows, width = vol_hbm.shape
    vpad = ratio_v.shape[1]
    my_d = lax.axis_index("depth")
    my_t = lax.axis_index("tile")
    has_prev = my_t > 0
    has_next = my_t < count_t - 1

    load_vol = pltpu.make_async_copy(vol_hbm, vol_v, load_sem.at[0])
    load_ps = pltpu.make_async_copy(ps_hbm, ps_v, load_sem.at[1])
    load_meas = pltpu.make_async_copy(meas_hbm, meas_v, load_sem.at[2])
    load_vol.start()
    load_ps.start()
    load_meas.start()

    def peer(k):
        flipped = my_d
        for bit in range(count_d.bit_length()):
            if (k >> bit) & 1:
                low = lax.rem(my_d // (1 << bit), 2)
                flipped = flipped + (1 << bit) - low * (2 << bit)
        return flipped

    others = sorted(range(1, count_d), key=lambda k: -k.bit_count())
    odd = lax.rem(my_t, 2) == 1

    barrier = pltpu.get_barrier_semaphore()

    def greet(k, move):
        pl.semaphore_signal(
            barrier, inc=1, device_id={"depth": peer(k), "tile": my_t + move}, device_id_type=MESH
        )

    for k in range(1, count_d):
        greet(k, 0)

    @pl.when(has_prev)
    def _():
        for k in range(count_d):
            greet(k, -1)

    @pl.when(has_next)
    def _():
        for k in range(count_d):
            greet(k, 1)

    @pl.when(jnp.logical_not(has_prev))
    def _():
        gathered[:, :radius] = jnp.zeros((count_d, radius, planes, width), BF16)
        ratio_v[:radius] = jnp.zeros((radius, vpad, width), BF16)

    @pl.when(jnp.logical_not(has_next))
    def _():
        gathered[:, radius + rows :] = jnp.zeros((count_d, radius, planes, width), BF16)
        ratio_v[radius + rows :] = jnp.zeros((radius, vpad, width), BF16)

    load_vol.wait()
    for y in range(rows):
        gathered[my_d, radius + y] = vol_v[:, y, :].astype(BF16)

    takes = (pl.ds(radius, rows), pl.ds(rows, radius), pl.ds(radius, radius))
    puts = (pl.ds(radius, rows), pl.ds(0, radius), pl.ds(radius + rows, radius))
    moves = (0, 1, -1)

    def gather_out(kind, k):
        return pltpu.make_async_remote_copy(
            src_ref=gathered.at[my_d, takes[kind]],
            dst_ref=gathered.at[my_d, puts[kind]],
            send_sem=gather_send.at[kind, k],
            recv_sem=gather_recv.at[kind, k],
            device_id={"depth": peer(k), "tile": my_t + moves[kind]},
            device_id_type=MESH,
        )

    def gather_in(kind, k):
        source = peer(k)
        return pltpu.make_async_remote_copy(
            src_ref=gathered.at[source, puts[kind]],
            dst_ref=gathered.at[source, puts[kind]],
            send_sem=gather_send.at[kind, k],
            recv_sem=gather_recv.at[kind, k],
            device_id={"depth": peer(k), "tile": my_t + moves[kind]},
            device_id_type=MESH,
        )

    pl.semaphore_wait(
        barrier,
        count_d * (1 + has_prev.astype(jnp.int32) + has_next.astype(jnp.int32)) - 1,
    )
    def forward(kind, k):
        source = peer(k)
        return pltpu.make_async_remote_copy(
            src_ref=gathered.at[source, takes[kind]],
            dst_ref=gathered.at[source, puts[kind]],
            send_sem=gather_send.at[kind, k],
            recv_sem=gather_recv.at[kind, k],
            device_id={"depth": my_d, "tile": my_t + moves[kind]},
            device_id_type=MESH,
        )

    even = jnp.logical_not(odd)

    def outer(ks):
        @pl.when(odd & has_next)
        def _():
            for k in ks:
                gather_out(1, k).start()

        @pl.when(even & has_prev)
        def _():
            for k in ks:
                gather_out(2, k).start()

    outer([others[0]])
    for k in others:
        gather_out(0, k).start()
    outer(others[1:] + [0])

    @pl.when(even & has_next)
    def _():
        gather_out(1, 0).start()

    @pl.when(odd)
    def _():
        gather_out(2, 0).start()

    load_ps.wait()
    row_id = lax.broadcasted_iota(jnp.int32, (vpad, views_all), 0)
    col_id = lax.broadcasted_iota(jnp.int32, (vpad, views_all), 1)
    pick = jnp.where((col_id == my_d * views + row_id) & (row_id < views), 1.0, 0.0).astype(BF16)
    for b in range(taps):
        table = ps_v[:, b].reshape(taps * planes_all, views_all)
        w_fwd[b * vpad : (b + 1) * vpad, :] = lax.dot_general(
            pick, table, (((1,), (1,)), ((), ())), preferred_element_type=F32
        ).astype(BF16)
    lanes = 128
    group = lanes // vpad
    from_id = lax.broadcasted_iota(jnp.int32, (views_all, lanes), 0)
    to_id = lax.broadcasted_iota(jnp.int32, (views_all, lanes), 1)
    for first in range(0, taps, group):
        placed = None
        for slot in range(min(group, taps - first)):
            offset = to_id - slot * vpad
            place = jnp.where(
                (from_id == my_d * views + offset) & (offset >= 0) & (offset < views), 1.0, 0.0
            ).astype(BF16)
            table = ps_v[taps - 1 - first - slot].reshape(taps * planes_all, views_all)
            term = jnp.dot(table, place, preferred_element_type=F32)
            placed = term if placed is None else placed + term
        w_back[:, first * vpad : first * vpad + lanes] = placed.astype(BF16)
    spread = jnp.zeros((planes_all, views_all), F32)
    for a in range(taps):
        for b in range(taps):
            spread = spread + ps_v[a, b].astype(F32)
    scale = 1.0 / jnp.sum(spread, axis=1, keepdims=True)
    load_meas.wait()

    for k in others:
        gather_in(0, k).wait_recv()

        @pl.when(even & has_next)
        def _():
            forward(1, k).start()

        @pl.when(odd)
        def _():
            forward(2, k).start()

    @pl.when(has_prev)
    def _():
        for k in range(count_d):
            gather_in(1, k).wait_recv()

    @pl.when(has_next)
    def _():
        for k in range(count_d):
            gather_in(2, k).wait_recv()

    for r in range(rows + 2 * radius):
        slab_v[r] = jnp.concatenate(
            [gathered[d, r].astype(F32) for d in range(count_d)], axis=0
        ).astype(BF16)

    def halo(up, piece):
        first, size = up_pieces[piece] if up else down_pieces[piece]
        take = pl.ds(radius + first, size)
        put = pl.ds(radius + first + (rows if up else -rows), size)
        return pltpu.make_async_remote_copy(
            src_ref=ratio_v.at[take],
            dst_ref=ratio_v.at[put],
            send_sem=halo_send.at[int(up), piece],
            recv_sem=halo_recv.at[int(up), piece],
            device_id={"depth": my_d, "tile": my_t - 1 if up else my_t + 1},
            device_id_type=MESH,
        )

    cut = (radius + 1) // 2
    up_pieces = ((0, cut), (cut, radius - cut))
    down_pieces = ((rows - radius, radius - cut), (rows - cut, cut))

    for y in range(rows):
        products = jnp.dot(
            w_fwd[...],
            slab_v[y : y + taps].reshape(taps * planes_all, width),
            preferred_element_type=F32,
        )
        projection = shifted_sum(products, taps, vpad, views, -1)
        ratio = meas_v[:, y, :] / projection
        if vpad > views:
            ratio = jnp.concatenate([ratio, jnp.zeros((vpad - views, width), F32)], axis=0)
        ratio_v[radius + y] = ratio.astype(BF16)
        ends_up = [i for i in range(2) if y + 1 == sum(up_pieces[i])]
        ends_down = [i for i in range(2) if y + 1 == sum(down_pieces[i])]
        if ends_up:
            @pl.when(has_prev)
            def _():
                halo(True, ends_up[0]).start()
        if ends_down:
            @pl.when(has_next)
            def _():
                halo(False, ends_down[0]).start()

    @pl.when(has_next)
    def _():
        halo(True, 0).wait_recv()
        halo(True, 1).wait_recv()

    @pl.when(has_prev)
    def _():
        halo(False, 0).wait_recv()
        halo(False, 1).wait_recv()

    half = rows // PIECES

    def part_out(piece, k):
        return pltpu.make_async_remote_copy(
            src_ref=part_v.at[peer(k), pl.ds(piece * half, half)],
            dst_ref=part_in.at[k, pl.ds(piece * half, half)],
            send_sem=sum_send.at[piece, k],
            recv_sem=sum_recv.at[piece, k],
            device_id={"depth": peer(k), "tile": my_t},
            device_id_type=MESH,
        )

    for y in range(rows):
        products = jnp.dot(
            w_back[:, : taps * vpad],
            ratio_v[y : y + taps].reshape(taps * vpad, width),
            preferred_element_type=F32,
        )
        back = shifted_sum(products, taps, planes_all, planes_all, 1) * scale
        back_v[y] = back
        for d in range(count_d):
            part_v[d, y] = back[d * planes : (d + 1) * planes]
        if (y + 1) % half == 0:
            for k in others:
                part_out(y // half, k).start()

    own = pl.ds(pl.multiple_of(my_d * planes, planes), planes)
    for piece in range(PIECES):
        for k in range(1, count_d):
            part_out(piece, k).wait_recv()
        for y in range(piece * half, (piece + 1) * half):
            total = back_v[y, own]
            for k in range(1, count_d):
                total = total + part_in[k, y]
            scaled_v[:, y, :] = total
    store = pltpu.make_async_copy(scaled_v, out_ref, load_sem.at[3])
    store.start()

    for k in range(1, count_d):
        gather_out(0, k).wait_send()
        for piece in range(PIECES):
            part_out(piece, k).wait_send()

    @pl.when(has_next)
    def _():
        for k in range(count_d):
            gather_out(1, k).wait_send()
        halo(False, 0).wait_send()
        halo(False, 1).wait_send()

    @pl.when(has_prev)
    def _():
        for k in range(count_d):
            gather_out(2, k).wait_send()
        halo(True, 0).wait_send()
        halo(True, 1).wait_send()

    store.wait()


def body(count_d, count_t, volume, measured, point_spread):
    planes, rows, width = volume.shape
    views = measured.shape[0]
    taps = point_spread.shape[0]
    radius = taps // 2
    planes_all = point_spread.shape[2]
    vpad = -(-views // 16) * 16
    group = 128 // vpad
    tall = rows + 2 * radius
    anywhere = pl.BlockSpec(memory_space=pl.ANY)
    scaled = pl.pallas_call(
        functools.partial(kernel, count_d, count_t, views),
        out_shape=jax.ShapeDtypeStruct(volume.shape, F32),
        in_specs=[pl.BlockSpec(memory_space=pltpu.HBM)] * 3,
        out_specs=anywhere,
        scratch_shapes=[
            pltpu.VMEM(volume.shape, F32),
            pltpu.VMEM(measured.shape, F32),
            pltpu.VMEM(point_spread.shape, BF16),
            pltpu.VMEM((count_d, tall, planes, width), BF16),
            pltpu.VMEM((tall, planes_all, width), BF16),
            pltpu.VMEM((taps * vpad, taps * planes_all), BF16),
            pltpu.VMEM((taps * planes_all, -(-taps // group) * 128), BF16),
            pltpu.VMEM((tall, vpad, width), BF16),
            pltpu.VMEM((count_d, rows, planes, width), F32),
            pltpu.VMEM((count_d, rows, planes, width), F32),
            pltpu.VMEM((rows, planes_all, width), F32),
            pltpu.VMEM(volume.shape, F32),
            pltpu.SemaphoreType.DMA((4,)),
            pltpu.SemaphoreType.DMA((3, count_d)),
            pltpu.SemaphoreType.DMA((3, count_d)),
            pltpu.SemaphoreType.DMA((2, 2)),
            pltpu.SemaphoreType.DMA((2, 2)),
            pltpu.SemaphoreType.DMA((PIECES, count_d)),
            pltpu.SemaphoreType.DMA((PIECES, count_d)),
        ],
        compiler_params=pltpu.CompilerParams(
            collective_id=0, has_side_effects=True, vmem_limit_bytes=32 * 2**20
        ),
    )(*(pltpu.with_memory_space_constraint(each, pltpu.HBM) for each in (volume, measured, point_spread)))
    return volume * scaled


def solution(mesh):
    in_specs = (P("depth", "tile", None), P("depth", "tile", None), P())
    out_specs = P("depth", "tile", None)
    run = functools.partial(body, mesh.shape["depth"], mesh.shape["tile"])
    return jax.shard_map(run, mesh=mesh, in_specs=in_specs, out_specs=out_specs, check_vma=False)
```

```python
import functools

import jax
import jax.numpy as jnp
from jax import lax
from jax.experimental import pallas as pl
from jax.experimental.pallas import tpu as pltpu
from jax.sharding import PartitionSpec as P

MESH = pl.DeviceIdType.MESH
F32 = jnp.float32
BF16 = jnp.bfloat16
PIECES = 4


def shifted_sum(products, taps, stride, used, sign):
    radius = taps // 2
    width = products.shape[1]
    lanes = lax.broadcasted_iota(jnp.int32, (used, width), 1)
    total = products[radius * stride : radius * stride + used]
    for b in range(taps):
        if b == radius:
            continue
        move = sign * (b - radius)
        piece = pltpu.roll(products[b * stride : b * stride + used], move % width, 1)
        keep = lanes >= move if move > 0 else lanes < width + move
        total = total + jnp.where(keep, piece, 0.0)
    return total


def kernel(
    count_d, count_t, views,
    vol_hbm, meas_hbm, ps_hbm, out_ref,
    vol_v, meas_v, ps_v, gathered, slab_v, w_fwd, w_back, ratio_v, part_v, part_in, back_v,
    scaled_v, meas_rows, load_sem, gather_send, gather_recv, halo_send, halo_recv, sum_send, sum_recv,
):
    taps = ps_hbm.shape[0]
    radius = taps // 2
    planes_all, views_all = ps_hbm.shape[2:]
    planes, rows, width = vol_hbm.shape
    vpad = ratio_v.shape[1]
    my_d = lax.axis_index("depth")
    my_t = lax.axis_index("tile")
    has_prev = my_t > 0
    has_next = my_t < count_t - 1

    load_vol = pltpu.make_async_copy(vol_hbm, vol_v, load_sem.at[0])
    load_ps = pltpu.make_async_copy(ps_hbm, ps_v, load_sem.at[1])
    load_meas = pltpu.make_async_copy(meas_hbm, meas_v, load_sem.at[2])
    load_vol.start()
    load_ps.start()
    load_meas.start()

    def peer(k):
        flipped = my_d
        for bit in range(count_d.bit_length()):
            if (k >> bit) & 1:
                low = lax.rem(my_d // (1 << bit), 2)
                flipped = flipped + (1 << bit) - low * (2 << bit)
        return flipped

    others = sorted(range(1, count_d), key=lambda k: -k.bit_count())
    odd = lax.rem(my_t, 2) == 1

    barrier = pltpu.get_barrier_semaphore()

    def greet(k, move):
        pl.semaphore_signal(
            barrier, inc=1, device_id={"depth": peer(k), "tile": my_t + move}, device_id_type=MESH
        )

    for k in range(1, count_d):
        greet(k, 0)

    @pl.when(has_prev)
    def _():
        for k in range(count_d):
            greet(k, -1)

    @pl.when(has_next)
    def _():
        for k in range(count_d):
            greet(k, 1)

    @pl.when(jnp.logical_not(has_prev))
    def _():
        gathered[:, :radius] = jnp.zeros((count_d, radius, planes, width), BF16)
        ratio_v[:radius] = jnp.zeros((radius, vpad, width), BF16)

    @pl.when(jnp.logical_not(has_next))
    def _():
        gathered[:, radius + rows :] = jnp.zeros((count_d, radius, planes, width), BF16)
        ratio_v[radius + rows :] = jnp.zeros((radius, vpad, width), BF16)

    load_vol.wait()
    for y in range(rows):
        gathered[my_d, radius + y] = vol_v[:, y, :].astype(BF16)

    takes = (pl.ds(radius, rows), pl.ds(rows, radius), pl.ds(radius, radius))
    puts = (pl.ds(radius, rows), pl.ds(0, radius), pl.ds(radius + rows, radius))
    moves = (0, 1, -1)

    def gather_out(kind, k):
        return pltpu.make_async_remote_copy(
            src_ref=gathered.at[my_d, takes[kind]],
            dst_ref=gathered.at[my_d, puts[kind]],
            send_sem=gather_send.at[kind, k],
            recv_sem=gather_recv.at[kind, k],
            device_id={"depth": peer(k), "tile": my_t + moves[kind]},
            device_id_type=MESH,
        )

    def gather_in(kind, k):
        source = peer(k)
        return pltpu.make_async_remote_copy(
            src_ref=gathered.at[source, puts[kind]],
            dst_ref=gathered.at[source, puts[kind]],
            send_sem=gather_send.at[kind, k],
            recv_sem=gather_recv.at[kind, k],
            device_id={"depth": peer(k), "tile": my_t + moves[kind]},
            device_id_type=MESH,
        )

    pl.semaphore_wait(
        barrier,
        count_d * (1 + has_prev.astype(jnp.int32) + has_next.astype(jnp.int32)) - 1,
    )
    def forward(kind, k):
        source = peer(k)
        return pltpu.make_async_remote_copy(
            src_ref=gathered.at[source, takes[kind]],
            dst_ref=gathered.at[source, puts[kind]],
            send_sem=gather_send.at[kind, k],
            recv_sem=gather_recv.at[kind, k],
            device_id={"depth": my_d, "tile": my_t + moves[kind]},
            device_id_type=MESH,
        )

    even = jnp.logical_not(odd)

    def outer(ks):
        @pl.when(odd & has_next)
        def _():
            for k in ks:
                gather_out(1, k).start()

        @pl.when(even & has_prev)
        def _():
            for k in ks:
                gather_out(2, k).start()

    outer([others[0]])
    for k in others:
        gather_out(0, k).start()
    outer(others[1:] + [0])

    @pl.when(even & has_next)
    def _():
        gather_out(1, 0).start()

    @pl.when(odd)
    def _():
        gather_out(2, 0).start()

    load_ps.wait()
    row_id = lax.broadcasted_iota(jnp.int32, (vpad, views_all), 0)
    col_id = lax.broadcasted_iota(jnp.int32, (vpad, views_all), 1)
    pick = jnp.where((col_id == my_d * views + row_id) & (row_id < views), 1.0, 0.0).astype(BF16)
    for b in range(taps):
        table = ps_v[:, b].reshape(taps * planes_all, views_all)
        w_fwd[b * vpad : (b + 1) * vpad, :] = lax.dot_general(
            pick, table, (((1,), (1,)), ((), ())), preferred_element_type=F32
        ).astype(BF16)
    lanes = 128
    group = lanes // vpad
    from_id = lax.broadcasted_iota(jnp.int32, (views_all, lanes), 0)
    to_id = lax.broadcasted_iota(jnp.int32, (views_all, lanes), 1)
    for first in range(0, taps, group):
        placed = None
        for slot in range(min(group, taps - first)):
            offset = to_id - slot * vpad
            place = jnp.where(
                (from_id == my_d * views + offset) & (offset >= 0) & (offset < views), 1.0, 0.0
            ).astype(BF16)
            table = ps_v[taps - 1 - first - slot].reshape(taps * planes_all, views_all)
            term = jnp.dot(table, place, preferred_element_type=F32)
            placed = term if placed is None else placed + term
        w_back[:, first * vpad : first * vpad + lanes] = placed.astype(BF16)
    spread = jnp.zeros((planes_all, views_all), F32)
    for a in range(taps):
        for b in range(taps):
            spread = spread + ps_v[a, b].astype(F32)
    scale = 1.0 / jnp.sum(spread, axis=1, keepdims=True)
    load_meas.wait()
    for y in range(rows):
        meas_rows[y] = jnp.where(odd, meas_v[:, rows - 1 - y, :], meas_v[:, y, :])

    for k in others:
        gather_in(0, k).wait_recv()

        @pl.when(even & has_next)
        def _():
            forward(1, k).start()

        @pl.when(odd)
        def _():
            forward(2, k).start()

    @pl.when(has_prev)
    def _():
        for k in range(count_d):
            gather_in(1, k).wait_recv()

    @pl.when(has_next)
    def _():
        for k in range(count_d):
            gather_in(2, k).wait_recv()

    for r in range(rows + 2 * radius):
        slab_v[r] = jnp.concatenate(
            [gathered[d, r].astype(F32) for d in range(count_d)], axis=0
        ).astype(BF16)

    def halo(up, piece):
        first, size = up_pieces[piece] if up else down_pieces[piece]
        take = pl.ds(radius + first, size)
        put = pl.ds(radius + first + (rows if up else -rows), size)
        return pltpu.make_async_remote_copy(
            src_ref=ratio_v.at[take],
            dst_ref=ratio_v.at[put],
            send_sem=halo_send.at[int(up), piece],
            recv_sem=halo_recv.at[int(up), piece],
            device_id={"depth": my_d, "tile": my_t - 1 if up else my_t + 1},
            device_id_type=MESH,
        )

    cut = (radius + 1) // 2
    up_pieces = ((0, cut), (cut, radius - cut))
    down_pieces = ((rows - radius, radius - cut), (rows - cut, cut))

    for y in range(rows):
        row = y + odd.astype(jnp.int32) * (rows - 1 - 2 * y)
        products = jnp.dot(
            w_fwd[...],
            slab_v[pl.ds(row, taps)].reshape(taps * planes_all, width),
            preferred_element_type=F32,
        )
        projection = shifted_sum(products, taps, vpad, views, -1)
        ratio = meas_rows[y] / projection
        if vpad > views:
            ratio = jnp.concatenate([ratio, jnp.zeros((vpad - views, width), F32)], axis=0)
        ratio_v[radius + row] = ratio.astype(BF16)
        ends_up = [i for i in range(2) if y + 1 == sum(up_pieces[i])]
        ends_down = [i for i in range(2) if y + 1 == sum(down_pieces[i])]
        if ends_up:
            @pl.when(even & has_prev)
            def _():
                halo(True, ends_up[0]).start()

            @pl.when(odd & has_next)
            def _():
                halo(False, 1 - ends_up[0]).start()
        if ends_down:
            @pl.when(even & has_next)
            def _():
                halo(False, ends_down[0]).start()

            @pl.when(odd)
            def _():
                halo(True, 1 - ends_down[0]).start()

    @pl.when(has_next)
    def _():
        halo(True, 0).wait_recv()
        halo(True, 1).wait_recv()

    @pl.when(has_prev)
    def _():
        halo(False, 0).wait_recv()
        halo(False, 1).wait_recv()

    half = rows // PIECES

    def part_out(piece, k):
        return pltpu.make_async_remote_copy(
            src_ref=part_v.at[peer(k), pl.ds(piece * half, half)],
            dst_ref=part_in.at[k, pl.ds(piece * half, half)],
            send_sem=sum_send.at[piece, k],
            recv_sem=sum_recv.at[piece, k],
            device_id={"depth": peer(k), "tile": my_t},
            device_id_type=MESH,
        )

    for y in range(rows):
        products = jnp.dot(
            w_back[:, : taps * vpad],
            ratio_v[y : y + taps].reshape(taps * vpad, width),
            preferred_element_type=F32,
        )
        back = shifted_sum(products, taps, planes_all, planes_all, 1) * scale
        back_v[y] = back
        for d in range(count_d):
            part_v[d, y] = back[d * planes : (d + 1) * planes]
        if (y + 1) % half == 0:
            for k in others:
                part_out(y // half, k).start()

    own = pl.ds(pl.multiple_of(my_d * planes, planes), planes)
    for piece in range(PIECES):
        for k in range(1, count_d):
            part_out(piece, k).wait_recv()
        for y in range(piece * half, (piece + 1) * half):
            total = back_v[y, own]
            for k in range(1, count_d):
                total = total + part_in[k, y]
            scaled_v[:, y, :] = total
    store = pltpu.make_async_copy(scaled_v, out_ref, load_sem.at[3])
    store.start()

    for k in range(1, count_d):
        gather_out(0, k).wait_send()
        for piece in range(PIECES):
            part_out(piece, k).wait_send()

    @pl.when(has_next)
    def _():
        for k in range(count_d):
            gather_out(1, k).wait_send()
        halo(False, 0).wait_send()
        halo(False, 1).wait_send()

    @pl.when(has_prev)
    def _():
        for k in range(count_d):
            gather_out(2, k).wait_send()
        halo(True, 0).wait_send()
        halo(True, 1).wait_send()

    store.wait()


def body(count_d, count_t, volume, measured, point_spread):
    planes, rows, width = volume.shape
    views = measured.shape[0]
    taps = point_spread.shape[0]
    radius = taps // 2
    planes_all = point_spread.shape[2]
    vpad = -(-views // 16) * 16
    group = 128 // vpad
    tall = rows + 2 * radius
    anywhere = pl.BlockSpec(memory_space=pl.ANY)
    scaled = pl.pallas_call(
        functools.partial(kernel, count_d, count_t, views),
        out_shape=jax.ShapeDtypeStruct(volume.shape, F32),
        in_specs=[pl.BlockSpec(memory_space=pltpu.HBM)] * 3,
        out_specs=anywhere,
        scratch_shapes=[
            pltpu.VMEM(volume.shape, F32),
            pltpu.VMEM(measured.shape, F32),
            pltpu.VMEM(point_spread.shape, BF16),
            pltpu.VMEM((count_d, tall, planes, width), BF16),
            pltpu.VMEM((tall, planes_all, width), BF16),
            pltpu.VMEM((taps * vpad, taps * planes_all), BF16),
            pltpu.VMEM((taps * planes_all, -(-taps // group) * 128), BF16),
            pltpu.VMEM((tall, vpad, width), BF16),
            pltpu.VMEM((count_d, rows, planes, width), F32),
            pltpu.VMEM((count_d, rows, planes, width), F32),
            pltpu.VMEM((rows, planes_all, width), F32),
            pltpu.VMEM(volume.shape, F32),
            pltpu.VMEM((rows, views, width), F32),
            pltpu.SemaphoreType.DMA((4,)),
            pltpu.SemaphoreType.DMA((3, count_d)),
            pltpu.SemaphoreType.DMA((3, count_d)),
            pltpu.SemaphoreType.DMA((2, 2)),
            pltpu.SemaphoreType.DMA((2, 2)),
            pltpu.SemaphoreType.DMA((PIECES, count_d)),
            pltpu.SemaphoreType.DMA((PIECES, count_d)),
        ],
        compiler_params=pltpu.CompilerParams(
            collective_id=0, has_side_effects=True, vmem_limit_bytes=32 * 2**20
        ),
    )(*(pltpu.with_memory_space_constraint(each, pltpu.HBM) for each in (volume, measured, point_spread)))
    return volume * scaled


def solution(mesh):
    in_specs = (P("depth", "tile", None), P("depth", "tile", None), P())
    out_specs = P("depth", "tile", None)
    run = functools.partial(body, mesh.shape["depth"], mesh.shape["tile"])
    return jax.shard_map(run, mesh=mesh, in_specs=in_specs, out_specs=out_specs, check_vma=False)
```
